512 devices in a mesh: seq: 64 (over y, z), tp: 8 (over x, core).
Axes of the slice: x: 4, y: 8, z: 8, core: 2. Of those that a mesh axis runs over, the one named last changes fastest.
Arguments:
- queries: bfloat16 [16384, 8192], P('seq', 'tp'), may hold values from -12 to 12
- kv_rows: bfloat16 [16384, 2048], P('seq', 'tp'), may hold values from -6 to 6
- vertical: int32 [64, 32], replicated, may hold values from 0 to 255, as said below
- slash: int32 [64, 8], replicated, may hold values from 0 to 11, as said below
Outputs:
- attended: bfloat16 [16384, 8192], P(('seq', 'tp'))
The draws below stay inside these ranges and needn't reach their ends.
Inputs may be any that keep to these rules, and one draw needn't show every extreme that they name: `vertical`: each row lists 32 distinct blocks in rising order and includes block 0 and block 255. The heads that share one key-value head list together exactly 48 distinct blocks. `slash`: each row lists 8 distinct offsets in rising order, the first 0 and the last 11.
All inputs are finite; a program needn't handle non-finite values.
Results may differ from the reference program's by a relative error of at most 0.0045.
Values may be sent and summed in bfloat16 or wider, within the bound.
A program may use at most 64 MiB of HBM per device.

```python
import jax
import jax.numpy as jnp
from jax import lax

HEADS = 64
KVH = 8
HEAD_SIZE = 128
BLK = 64
NSL = 8
SEQ = 16384
NB = 256
BLOCKS_PER_INDEX = 4
SMAX = 11
VERTICAL_COUNT = 32
GV = 48
N_SEQ = 64


def draw_queries(key, part):
    inner = jax.random.fold_in(key, 1)
    base = jax.random.truncated_normal(inner, -6.0, 6.0, (SEQ, HEADS, HEAD_SIZE), jnp.float32)
    return base.reshape(SEQ, HEADS * HEAD_SIZE).astype(jnp.bfloat16)


def draw_kv_rows(key, part):
    inner = jax.random.fold_in(key, 2)
    base = jax.random.truncated_normal(inner, -6.0, 6.0, (SEQ, KVH, 2, HEAD_SIZE), jnp.float32)
    return base.reshape(SEQ, KVH * 2 * HEAD_SIZE).astype(jnp.bfloat16)


def draw_vertical(key, part):
    group = HEADS // KVH
    middle_count = GV - 2
    gkeys = jax.random.split(jax.random.fold_in(key, 3), KVH)
    picks = jax.vmap(lambda sub: jax.random.permutation(sub, NB - 2))(gkeys)
    middle = jnp.sort(picks[:, :middle_count].astype(jnp.int32) + 1, axis=1)
    okeys = jax.random.split(jax.random.fold_in(key, 4), KVH)
    orders = jax.vmap(lambda sub: jax.random.permutation(sub, middle_count))(okeys).astype(jnp.int32)
    heads = jnp.arange(HEADS, dtype=jnp.int32)
    owner = heads // group
    member = heads % group
    starts = member * middle_count // group
    steps = jnp.arange(VERTICAL_COUNT - 2, dtype=jnp.int32)
    places = (starts[:, None] + steps[None, :]) % middle_count
    slots = jnp.take_along_axis(orders[owner], places, axis=1)
    taken = jnp.take_along_axis(middle[owner], slots, axis=1)
    firsts = jnp.zeros((HEADS, 1), jnp.int32)
    lasts = jnp.full((HEADS, 1), NB - 1, jnp.int32)
    return jnp.sort(jnp.concatenate([firsts, taken, lasts], axis=1), axis=1).astype(jnp.int32)


def draw_slash(key, part):
    subkeys = jax.random.split(jax.random.fold_in(key, 5), HEADS)
    shuffled = jax.vmap(lambda sub: jax.random.permutation(sub, SMAX - 1))(subkeys) + 1
    firsts = jnp.zeros((HEADS, 1), jnp.int32)
    lasts = jnp.full((HEADS, 1), SMAX, jnp.int32)
    rows = jnp.concatenate([firsts, shuffled[:, :NSL - 2].astype(jnp.int32), lasts], axis=1)
    return jnp.sort(rows, axis=1).astype(jnp.int32)


def setup_inputs(seed: int = 0) -> dict:
    splits = jax.random.split(jax.random.key(seed), 5)
    return {
        "queries": draw_queries(jax.random.fold_in(splits[4], 71), 0),
        "kv_rows": draw_kv_rows(jax.random.fold_in(splits[4], 71), 0),
        "vertical": draw_vertical(jax.random.fold_in(splits[4], 71), 0),
        "slash": draw_slash(jax.random.fold_in(splits[4], 71), 0),
    }


def key_mask(bids, vertical_row, srow):
    dist = bids[:, None] - vertical_row[None, :]
    hit = jnp.any(dist[:, :, None] == srow[None, None, :], axis=2)
    live_v = jnp.logical_and(dist >= 0, jnp.logical_not(hit))
    live_s = (bids[:, None] - srow[None, :]) >= 0
    live = jnp.concatenate([live_v, live_s], axis=1)
    diag = jnp.concatenate([jnp.zeros(vertical_row.shape, bool), srow == 0])
    rows = jnp.arange(BLK, dtype=jnp.int32)
    lower = rows[None, :] <= rows[:, None]
    return live[:, None, :, None] & (jnp.logical_not(diag)[None, None, :, None] | lower[None, :, None, :])


def attend(query_block, key_value_block, bids, vertical_row, srow):
    key_rows = key_value_block[..., :HEAD_SIZE].astype(jnp.float32)
    value_rows = key_value_block[..., HEAD_SIZE:].astype(jnp.float32)
    logit_matrix = jnp.einsum("unz,usyz->unsy", query_block.astype(jnp.float32), key_rows) * (1.0 / (HEAD_SIZE ** 0.5))
    mask = key_mask(bids, vertical_row, srow)
    logit_matrix = jnp.where(mask, logit_matrix, -1e30)
    top = jnp.max(logit_matrix, axis=(2, 3), keepdims=True)
    weights = jnp.where(mask, jnp.exp(logit_matrix - top), 0.0)
    total = jnp.sum(weights, axis=(2, 3))
    probabilities = lax.optimization_barrier(weights.astype(jnp.bfloat16))
    weighted_sum = jnp.einsum("wtef,wefs->wts", probabilities.astype(jnp.float32), value_rows)
    return (weighted_sum / total[..., None]).astype(jnp.bfloat16)


def reference(queries, kv_rows, vertical, slash):
    group = HEADS // KVH
    qall = queries.reshape(SEQ, HEADS, HEAD_SIZE)
    index_table = kv_rows.reshape(NB, BLK, KVH, 2 * HEAD_SIZE)

    def one_head(head):
        key_value_head = head // group
        vertical_row = vertical[head]
        srow = slash[head]
        qhead = lax.dynamic_index_in_dim(qall, head, 1, keepdims=False)
        qhead = qhead.reshape(N_SEQ, BLOCKS_PER_INDEX, BLK, HEAD_SIZE)

        def one_span(item):
            qspan, start = item
            bids = start + jnp.arange(BLOCKS_PER_INDEX, dtype=jnp.int32)
            vertical_index = jnp.broadcast_to(vertical_row[None, :], (BLOCKS_PER_INDEX, VERTICAL_COUNT))
            slash_index = jnp.clip(bids[:, None] - srow[None, :], 0, NB - 1)
            block_index = jnp.concatenate([vertical_index, slash_index], axis=1).astype(jnp.int32)
            key_value_block = index_table[block_index, :, key_value_head]
            return attend(qspan, key_value_block, bids, vertical_row, srow)

        starts = jnp.arange(N_SEQ, dtype=jnp.int32) * BLOCKS_PER_INDEX
        out = lax.map(one_span, (qhead, starts))
        return out.reshape(SEQ, HEAD_SIZE)

    result = lax.map(one_head, jnp.arange(HEADS, dtype=jnp.int32))
    return jnp.transpose(result, (1, 0, 2)).reshape(SEQ, HEADS * HEAD_SIZE)
```

```python
import jax
import jax.numpy as jnp
from jax import lax
from jax.experimental import pallas as pl
from jax.experimental.pallas import tpu as pltpu
from jax.sharding import PartitionSpec as P

HEAD_SIZE = 128
BLK = 64
SIDE = 8
NPIECE = 8
GV = 48
HEADS_LOC = 8
NTP = 8
MASKED = -1e30
MESH = pl.DeviceIdType.MESH
LOG2E = 1.4426950408889634


def kv_kernel(sel_ref, kv_ref, pk_ref, pv_ref, wk_ref, wv_ref, p2k, p2v,
              a2a_send, a2a_recv, ring2_send, ring2_recv, ring3_send, ring3_recv,
              win_send, win_recv, loc_sem):
    seq = lax.axis_index("seq")
    y, z = seq // SIDE, seq % SIDE

    def at(yy, zz):
        return {"seq": (yy % SIDE) * SIDE + zz % SIDE}

    nxt = {"seq": (seq + 1) % (SIDE * SIDE)}
    prv = {"seq": (seq + SIDE * SIDE - 1) % (SIDE * SIDE)}

    barrier = pltpu.get_barrier_semaphore()
    for j in range(1, SIDE):
        pl.semaphore_signal(barrier, inc=1, device_id=at(y + j, z), device_id_type=MESH)
        pl.semaphore_signal(barrier, inc=1, device_id=at(y, z + j), device_id_type=MESH)
    pl.semaphore_signal(barrier, inc=1, device_id=nxt, device_id_type=MESH)
    pl.semaphore_signal(barrier, inc=1, device_id=prv, device_id_type=MESH)

    own = [
        pltpu.make_async_copy(kv_ref.at[:, y, :, 0:128], p2k.at[z, y], loc_sem.at[0]),
        pltpu.make_async_copy(kv_ref.at[:, z, :, 128:256], p2v.at[y, z], loc_sem.at[1]),
        pltpu.make_async_copy(kv_ref.at[:, :, :, 0:128], wk_ref.at[3], loc_sem.at[2]),
        pltpu.make_async_copy(kv_ref.at[:, :, :, 128:256], wv_ref.at[3], loc_sem.at[3]),
    ]
    for copy in own:
        copy.start()
    pl.semaphore_wait(barrier, 2 * (SIDE - 1) + 2)

    sends = []

    def remote(src, dst, ssem, rsem, dev):
        copy = pltpu.make_async_remote_copy(
            src_ref=src, dst_ref=dst, send_sem=ssem, recv_sem=rsem, device_id=dev,
            device_id_type=MESH)
        copy.start()
        sends.append(copy)
        return copy

    first = []
    for j in (4, 3, 5, 2, 6, 1, 7):
        p = (y + j) % SIDE
        first.append(remote(kv_ref.at[:, p, :, 0:128], p2k.at[z, y],
                            a2a_send.at[0, j - 1], a2a_recv.at[0, j - 1], at(y + j, z)))
        q = (z + j) % SIDE
        first.append(remote(kv_ref.at[:, q, :, 128:256], p2v.at[y, z],
                            a2a_send.at[1, j - 1], a2a_recv.at[1, j - 1], at(y, z + j)))
    for copy in own:
        copy.wait()
    window = []
    for half, ref in ((0, wk_ref), (1, wv_ref)):
        window.append(remote(ref.at[3], ref.at[2], win_send.at[half, 0], win_recv.at[half, 0], nxt))
    for copy in first:
        copy.wait_recv()

    def ring(bufs, sems_s, sems_r, middle):
        def send(index, sign, k):
            buf, c, dev = bufs[index]
            src = (c - sign * (k - 1)) % SIDE
            d = 0 if sign > 0 else 1
            return remote(buf.at[src], buf.at[src], sems_s.at[index, d, k - 1],
                          sems_r.at[index, d, k - 1], dev(sign))

        live = {}
        for index in (0, 1):
            for sign in (1, -1):
                live[index, sign] = send(index, sign, 1)
        for k in range(1, 5):
            for index in (0, 1):
                for sign in (-1, 1):
                    if (index, sign) in live:
                        live[index, sign].wait_recv()
                        if k < (3 if sign > 0 else 4):
                            live[index, sign] = send(index, sign, k + 1)
                        else:
                            del live[index, sign]
            middle(k)

    def forward_window(k):
        if k in (1, 2):
            for half, ref in ((0, wk_ref), (1, wv_ref)):
                window[-2].wait_recv()
                window.append(remote(ref.at[3 - k], ref.at[2 - k], win_send.at[half, k],
                                     win_recv.at[half, k], nxt))

    along_y = lambda sign: at(y + SIDE + sign, z)
    along_z = lambda sign: at(y, z + SIDE + sign)
    ring([(p2k, z, along_z), (p2v, y, along_y)], ring2_send, ring2_recv, forward_window)

    @pl.loop(0, GV)
    def _(s):
        b = sel_ref[s]
        by, bz, bi = b // (4 * SIDE), (b // 4) % SIDE, b % 4
        pk_ref[y, s] = p2k[bz, by, bi]
        pv_ref[z, s] = p2v[by, bz, bi]

    ring([(pk_ref, y, along_y), (pv_ref, z, along_z)], ring3_send, ring3_recv, lambda k: None)
    for copy in window[-2:]:
        copy.wait_recv()
    for copy in sends:
        copy.wait_send()


def attend_kernel(q_ref, bias_ref, k_ref, v_ref, wk_ref, wv_ref, out_ref, attn, send, recv, loc_sem):
    seq = lax.axis_index("seq")
    tp = lax.axis_index("tp")
    barrier = pltpu.get_barrier_semaphore()
    for j in range(1, NTP):
        pl.semaphore_signal(barrier, inc=1, device_id={"tp": (tp + j) % NTP}, device_id_type=MESH)
    pl.semaphore_wait(barrier, NTP - 1)
    scale = LOG2E / HEAD_SIZE**0.5
    rows = attn.shape[1]
    own = 4 * BLK
    chunk = 768

    def pattern(shape, value):
        lane = lax.broadcasted_iota(jnp.int32, shape, 1)
        row = lax.broadcasted_iota(jnp.int32, shape, 0)
        return jnp.where(lane == value(row), 1.0, 0.0).astype(jnp.bfloat16)

    def contract(a, b):
        return lax.dot_general(a, b, (((1,), (1,)), ((), ())), preferred_element_type=jnp.float32)

    def one_head(h, carry):
        lanes = pl.ds(pl.multiple_of(h * HEAD_SIZE, HEAD_SIZE), HEAD_SIZE)
        q = q_ref[:, lanes]
        bias = bias_ref[h]
        qbias = jnp.concatenate(
            [jnp.broadcast_to(bias[b:b + 1], (BLK, HEAD_SIZE)) for b in range(4)], axis=0)
        qa = jnp.concatenate([q, qbias.astype(jnp.bfloat16)], axis=1)
        ones = jnp.ones((4 * own, HEAD_SIZE), jnp.bfloat16)

        wk = wk_ref[...]
        ka = jnp.concatenate([wk, pattern((4 * own, HEAD_SIZE), lambda r: GV + r // BLK)], axis=1)
        s = contract(qa, ka)
        qrow = lax.broadcasted_iota(jnp.int32, (own, own), 0)
        kcol = lax.broadcasted_iota(jnp.int32, (own, own), 1)
        s = jnp.concatenate([s[:, :3 * own], jnp.where(kcol > qrow, MASKED, s[:, 3 * own:])], axis=1)
        m = jnp.max(s, axis=1, keepdims=True)
        p = jnp.exp2((s - m) * scale).astype(jnp.bfloat16)
        acc = jnp.dot(p, jnp.concatenate([wv_ref[...], ones], axis=1), preferred_element_type=jnp.float32)
        for c in range(NPIECE * GV * 8 // chunk):
            k = k_ref[c * chunk:(c + 1) * chunk]
            v = v_ref[c * chunk:(c + 1) * chunk]
            ka = jnp.concatenate([k, pattern((chunk, HEAD_SIZE), lambda r: (r // 8) % GV)], axis=1)
            s = contract(qa, ka)
            m_new = jnp.maximum(m, jnp.max(s, axis=1, keepdims=True))
            alpha = jnp.exp2((m - m_new) * scale)
            p = jnp.exp2((s - m_new) * scale).astype(jnp.bfloat16)
            acc = acc * alpha + jnp.dot(p, jnp.concatenate([v, ones[:chunk]], axis=1),
                                        preferred_element_type=jnp.float32)
            m = m_new
        attn[:, :, lanes] = (acc[:, :HEAD_SIZE] / acc[:, HEAD_SIZE:]).astype(jnp.bfloat16).reshape(
            NTP, rows, HEAD_SIZE)
        for j in range(1, NTP):
            t = (tp + j) % NTP
            pltpu.make_async_remote_copy(
                src_ref=attn.at[t, :, lanes],
                dst_ref=out_ref.at[tp, :, lanes],
                send_sem=send.at[j - 1], recv_sem=recv.at[j - 1],
                device_id={"tp": t}, device_id_type=MESH).start()
        return carry

    lax.fori_loop(0, HEADS_LOC, one_head, 0)
    mine = pltpu.make_async_copy(attn.at[tp], out_ref.at[tp], loc_sem)
    mine.start()
    mine.wait()
    for j in range(1, NTP):
        t = (tp + j) % NTP
        copy = pltpu.make_async_remote_copy(
            src_ref=attn.at[t], dst_ref=out_ref.at[tp], send_sem=send.at[j - 1],
            recv_sem=recv.at[j - 1], device_id={"tp": t}, device_id_type=MESH)
        copy.wait_send()
        copy.wait_recv()


def tables(vert, srow, first):
    ids = jnp.arange(256, dtype=jnp.int32)
    present = jnp.any(vert.reshape(-1, 1) == ids[None, :], axis=0)
    rank = jnp.sum((present[None, :] & (ids[None, :] <= ids[:, None])).astype(jnp.int32), axis=1)
    slot = jnp.arange(GV, dtype=jnp.int32)
    sel = jnp.sum(jnp.where(present[None, :] & (rank[None, :] == slot[:, None] + 1), ids[None, :], 0), axis=1)
    bids = first + jnp.arange(4, dtype=jnp.int32)
    listed = jnp.any(vert[:, None, :] == sel[None, :, None], axis=2)
    dist = bids[:, None] - sel[None, :]
    hit = jnp.any(dist[None, :, :, None] == srow[:, None, None, :], axis=3)
    live_v = listed[:, None, :] & (dist >= 0)[None] & jnp.logical_not(hit)
    w = jnp.arange(16, dtype=jnp.int32)
    offset = jnp.arange(4, dtype=jnp.int32)[:, None] + 12 - w[None, :]
    live_w = jnp.any(offset[None, :, :, None] == srow[:, None, None, :], axis=3)
    live_w = live_w & (first - 12 + w >= 0)[None, None, :]
    live = jnp.concatenate([live_v, live_w], axis=2)
    bias = jnp.where(live, 0.0, MASKED).astype(jnp.float32)
    return sel, jnp.concatenate([bias, jnp.zeros_like(bias)], axis=2)


def per_device(queries, kv_rows, vertical, slash):
    tok = queries.shape[0]
    seq_pos = lax.axis_index("seq")
    tp_pos = lax.axis_index("tp")
    vert = lax.dynamic_slice_in_dim(vertical, tp_pos * HEADS_LOC, HEADS_LOC, 0)
    srow = lax.dynamic_slice_in_dim(slash, tp_pos * HEADS_LOC, HEADS_LOC, 0)
    sel, bias = tables(vert, srow, seq_pos * 4)
    vmem = pl.BlockSpec(memory_space=pltpu.VMEM)
    dma = pltpu.SemaphoreType.DMA
    pk, pv, wk, wv = pl.pallas_call(
        kv_kernel,
        out_shape=[jax.ShapeDtypeStruct((NPIECE, GV, 8, 128), jnp.bfloat16)] * 2
        + [jax.ShapeDtypeStruct((4, 4, 8, 8, 128), jnp.bfloat16)] * 2,
        in_specs=[pl.BlockSpec(memory_space=pltpu.SMEM), vmem],
        out_specs=[vmem] * 4,
        scratch_shapes=[
            pltpu.VMEM((SIDE, SIDE, 4, 8, 128), jnp.bfloat16),
            pltpu.VMEM((SIDE, SIDE, 4, 8, 128), jnp.bfloat16),
            dma((2, 7)), dma((2, 7)), dma((2, 2, 4)), dma((2, 2, 4)), dma((2, 2, 4)), dma((2, 2, 4)),
            dma((2, 3)), dma((2, 3)), dma((4,)),
        ],
        compiler_params=pltpu.CompilerParams(collective_id=0, has_side_effects=True),
        name="kv_exchange",
    )(sel, kv_rows.reshape(4, NPIECE, 8, 256))
    rows = tok // NTP
    out = pl.pallas_call(
        attend_kernel,
        out_shape=jax.ShapeDtypeStruct((NTP, rows, HEADS_LOC * HEAD_SIZE), jnp.bfloat16),
        in_specs=[vmem] * 6,
        out_specs=vmem,
        scratch_shapes=[
            pltpu.VMEM((NTP, rows, HEADS_LOC * HEAD_SIZE), jnp.bfloat16),
            dma((7,)), dma((7,)), dma(()),
        ],
        compiler_params=pltpu.CompilerParams(collective_id=1, has_side_effects=True),
        name="attend",
    )(queries, bias, pk.reshape(-1, 128), pv.reshape(-1, 128), wk.reshape(-1, 128), wv.reshape(-1, 128))
    return jnp.transpose(out, (1, 0, 2)).reshape(rows, NTP * HEADS_LOC * HEAD_SIZE)


def solution(mesh):
    return jax.shard_map(
        per_device,
        mesh=mesh,
        in_specs=(P("seq", "tp"), P("seq", "tp"), P(), P()),
        out_specs=P(("seq", "tp"), None),
        check_vma=False,
    )
```
